32 devices in a mesh: dp: 8 (over y, x, core), tensor: 4 (over z).
Axes of the slice: x: 2, y: 2, z: 4, core: 2. Of those that a mesh axis runs over, the one named last changes fastest.
Arguments:
- block_input: bfloat16 [2560, 1024], P('dp'), may hold values from -6 to 6
- segment_ids: int32 [2560], P('dp'), may hold values from -1 to 2559, as said below
- norm_attn: float32 [1024], replicated, may hold values from 0.5 to 1.5
- w_query: bfloat16 [1024, 512], P(None, 'tensor'), may hold values from -0.1875 to 0.1875
- w_key: bfloat16 [1024, 512], P(None, 'tensor'), may hold values from -0.1875 to 0.1875
- w_value: bfloat16 [1024, 1024], P(None, 'tensor'), may hold values from -0.1875 to 0.1875
- w_outgate: bfloat16 [1024, 1024], P(None, 'tensor'), may hold values from -0.1875 to 0.1875
- w_lowrank: bfloat16 [1024, 16], replicated, may hold values from -0.1875 to 0.1875
- w_forget: bfloat16 [16, 512], P(None, 'tensor'), may hold values from -1.5 to 1.5
- forget_bias: float32 [512], P('tensor'), may hold values from -1 to 5
- norm_group: float32 [256], replicated, may hold values from 0.5 to 1.5
- w_output: bfloat16 [1024, 1024], P('tensor'), may hold values from -0.25 to 0.25
- norm_ffn: float32 [1024], replicated, may hold values from 0.5 to 1.5
- w_gate: bfloat16 [1024, 2816], P(None, 'tensor'), may hold values from -0.1875 to 0.1875
- w_up: bfloat16 [1024, 2816], P(None, 'tensor'), may hold values from -0.1875 to 0.1875
- w_down: bfloat16 [2816, 1024], P('tensor'), may hold values from -0.109375 to 0.109375
- out_grad: bfloat16 [2560, 1024], P('dp'), may hold values from -6 to 6
Outputs:
- block_output: bfloat16 [2560, 1024], P('dp')
- input_grad: bfloat16 [2560, 1024], P('dp')
- grad_norm_attn: float32 [1024], P('dp')
- grad_w_query: float32 [1024, 512], P('dp', 'tensor')
- grad_w_key: float32 [1024, 512], P('dp', 'tensor')
- grad_w_value: float32 [1024, 1024], P('dp', 'tensor')
- grad_w_outgate: float32 [1024, 1024], P('dp', 'tensor')
- grad_w_lowrank: float32 [1024, 16], P('dp')
- grad_w_forget: float32 [16, 512], P(None, 'tensor')
- grad_forget_bias: float32 [512], P('tensor')
- grad_norm_group: float32 [256], P('dp')
- grad_w_output: float32 [1024, 1024], P('tensor', 'dp')
- grad_norm_ffn: float32 [1024], P('dp')
- grad_w_gate: float32 [1024, 2816], P('dp', 'tensor')
- grad_w_up: float32 [1024, 2816], P('dp', 'tensor')
- grad_w_down: float32 [2816, 1024], P('tensor', 'dp')
The draws below stay inside these ranges and needn't reach their ends.
Inputs may be any that keep to these rules, and one draw needn't show every extreme that they name: `segment_ids`: within each aligned block of 320 slots (block r), the used slots come first; each used slot carries the global index of the last slot of its segment, so the numbers are non-decreasing and lie between 320 * r and 320 * r + 319; the remaining slots of the block are -1. At least half of every block is used, the last block is used in full.
All inputs are finite; a program needn't handle non-finite values.
Results may differ from the reference program's by a relative error of at most 0.018.
Values sent between devices are 32-bit elements; how exact they have to be, the bound alone decides.
No kernel may reach another device: no remote copies, remote signals or barrier semaphores. Data moves between devices by JAX's collectives and lax.ppermute only.
A program may use at most 128 MiB of HBM per device.

```python
import jax
import jax.numpy as jnp
from jax import lax

D = 1024
KH = 128
VH = 256
RANK = 16
FF = 2816
SPAN = 64
TOK_DEV = 320
KEYS = 512
VALS = 1024
TOKENS = 2560


def draw_segment_ids(key, part):
    ranks = TOKENS // TOK_DEV
    key_count, key_full, key_start = jax.random.split(key, 3)
    live_count = jax.random.randint(key_count, (ranks,), TOK_DEV // 2, TOK_DEV + 1)
    full_rank = jax.random.randint(key_full, (), 0, ranks)
    rank_index = jnp.arange(ranks, dtype=jnp.int32)
    live_count = jnp.where((rank_index == full_rank) | (rank_index == ranks - 1), TOK_DEV, live_count)
    position = jnp.arange(TOK_DEV, dtype=jnp.int32)
    starts = jax.random.randint(key_start, (ranks, TOK_DEV), 0, 64) == 0
    starts = starts | (position[None, :] == 0)
    next_start = jnp.concatenate([starts[:, 1:], jnp.ones((ranks, 1), dtype=bool)], axis=1)
    bound_here = next_start | (position[None, :] == live_count[:, None] - 1)
    candidate = jnp.where(bound_here, position[None, :], TOK_DEV).astype(jnp.int32)
    ends = lax.cummin(candidate, axis=1, reverse=True)
    ids = jnp.where(position[None, :] < live_count[:, None], ends + rank_index[:, None] * TOK_DEV, -1)
    return ids.reshape(TOKENS).astype(jnp.int32)


def block_levels(own_key, dims, shards, low, largest):
    def one(dim, shards_of):
        draws = jax.random.uniform(jax.random.fold_in(jax.random.fold_in(own_key, 6), dim), (shards_of,), jnp.float32, low / len(shards), largest / len(shards))
        return jnp.repeat(jnp.exp(draws), dims[dim] // shards_of).reshape((-1,) + (1,) * (len(dims) - dim - 1))

    level = one(*shards[0])
    for cut in shards[1:]:
        level = level * one(*cut)
    return level


def bell_draw(stream_key, dims, width, most, pieces=(), kind=jnp.bfloat16):
    values = width * jax.random.normal(stream_key, dims, jnp.float32)
    if pieces:
        values = values * block_levels(stream_key, dims, pieces, -0.22, 0.18)
    return jnp.clip(values, -most, most).astype(kind)


def setup_inputs(seed: int = 0) -> dict:
    key_list = jax.random.split(jax.random.key(seed), 18)
    block_input = bell_draw(key_list[0], (TOKENS, D), 1.0, 6.0, ((0, 8),))
    segment_ids = draw_segment_ids(jax.random.fold_in(key_list[17], 71), 0)
    norm_attn = jnp.clip(1.0 + 0.1 * jax.random.normal(key_list[2], (D,), jnp.float32), 0.5, 1.5)
    w_query = bell_draw(key_list[3], (D, KEYS), D ** -0.5, 0.1875, ((1, 4),))
    w_key = bell_draw(key_list[4], (D, KEYS), D ** -0.5, 0.1875, ((1, 4),))
    w_value = bell_draw(key_list[5], (D, VALS), D ** -0.5, 0.1875, ((1, 4),))
    w_outgate = bell_draw(key_list[6], (D, VALS), D ** -0.5, 0.1875, ((1, 4),))
    w_lowrank = bell_draw(key_list[7], (D, RANK), D ** -0.5, 0.1875)
    w_forget = bell_draw(key_list[8], (RANK, KEYS), RANK ** -0.5, 1.5, ((1, 4),))
    forget_bias = jnp.clip(-1.0 + 6.0 * jax.random.uniform(key_list[9], (KEYS,), jnp.float32) ** block_levels(key_list[9], (KEYS,), ((0, 4),), -0.2, 0.2), -1.0, 5.0)
    norm_group = jnp.clip(1.0 + 0.1 * jax.random.normal(key_list[10], (VH,), jnp.float32), 0.5, 1.5)
    w_output = bell_draw(key_list[11], (VALS, D), (VALS // 2) ** -0.5, 0.25, ((0, 4),))
    norm_ffn = jnp.clip(1.0 + 0.1 * jax.random.normal(key_list[12], (D,), jnp.float32), 0.5, 1.5)
    w_gate = bell_draw(key_list[13], (D, FF), D ** -0.5, 0.1875, ((1, 4),))
    w_up = bell_draw(key_list[14], (D, FF), D ** -0.5, 0.1875, ((1, 4),))
    w_down = bell_draw(key_list[15], (FF, D), FF ** -0.5, 0.109375, ((0, 4),))
    out_grad = bell_draw(key_list[16], (TOKENS, D), 1.0, 6.0, ((0, 8),))
    return dict(block_input=block_input, segment_ids=segment_ids, norm_attn=norm_attn, w_query=w_query, w_key=w_key, w_value=w_value, w_outgate=w_outgate, w_lowrank=w_lowrank, w_forget=w_forget, forget_bias=forget_bias, norm_group=norm_group, w_output=w_output, norm_ffn=norm_ffn, w_gate=w_gate, w_up=w_up, w_down=w_down, out_grad=out_grad)


norm_eps = 1e-06
group_eps = 0.1
gate_norm = 16.0
exact_prec = lax.Precision.HIGHEST

def matmul(left, right):
    return jnp.dot(left, right, preferred_element_type=jnp.float32)

def exact_matmul(left, right):
    return jnp.dot(left.astype(jnp.float32), right.astype(jnp.float32), precision=exact_prec, preferred_element_type=jnp.float32)

def span_step(carried, inputs_now):
    memory, seg_prev = carried
    queries, key_vecs, value_vecs, log_decay, segment = inputs_now
    length = segment.shape[0]
    cumulative = jnp.cumsum(log_decay, axis=1)
    row_index = lax.broadcasted_iota(jnp.int32, (length, length), 0)
    col_index = lax.broadcasted_iota(jnp.int32, (length, length), 1)
    same_seg = (row_index >= col_index) & (segment[:, None] == segment[None, :])
    gap_log = cumulative[:, :, None, :] - cumulative[:, None, :, :]
    decays = jnp.exp(jnp.where(same_seg[None, :, :, None], gap_log, -10000.0))
    scores = jnp.einsum('htd,hsd,htsd->hts', queries, key_vecs, decays, precision=exact_prec)
    inside = jnp.einsum('hts,hsv->htv', scores, value_vecs, precision=exact_prec)
    keep_mask = (segment == seg_prev).astype(jnp.float32)
    carried_out = jnp.einsum('htd,hdv->htv', queries * jnp.exp(cumulative), memory, precision=exact_prec)
    result = inside + carried_out * keep_mask[None, :, None]
    last_seg = segment[length - 1]
    final_log = cumulative[:, length - 1, :]
    in_last = (segment == last_seg).astype(jnp.float32)
    weighted = key_vecs * jnp.exp(final_log[:, None, :] - cumulative) * in_last[None, :, None]
    kept_flag = (last_seg == seg_prev).astype(jnp.float32)
    memory = kept_flag * jnp.exp(final_log)[:, :, None] * memory + jnp.einsum('hsd,hsv->hdv', weighted, value_vecs, precision=exact_prec)
    return ((memory, last_seg), result)

def attend(queries, key_vecs, value_vecs, log_decay, segment_ids):
    total_rows = queries.shape[0]
    head_count = queries.shape[1] // KH
    blocks = total_rows // SPAN

    def to_blocks(array, columns):
        return array.reshape(blocks, SPAN, head_count, columns).transpose(0, 2, 1, 3)
    inputs_all = (to_blocks(queries * KH ** (-0.5), KH), to_blocks(key_vecs, KH), to_blocks(value_vecs, VH), to_blocks(log_decay, KH), segment_ids.reshape(blocks, SPAN).astype(jnp.int32))
    initial = (jnp.zeros((head_count, KH, VH), jnp.float32), jnp.array(-2, jnp.int32))
    _, results = lax.scan(jax.checkpoint(span_step), initial, inputs_all)
    return results.transpose(0, 2, 1, 3).reshape(total_rows, head_count * VH)

def gated(mixed, outgate, gain):
    total_rows = mixed.shape[0]
    head_count = mixed.shape[1] // VH
    per_head = mixed.reshape(total_rows, head_count, VH)
    scaled = per_head * lax.rsqrt(lax.optimization_barrier(jnp.mean(per_head * per_head, axis=-1, keepdims=True)) + group_eps) * gain
    gate_heads = outgate.reshape(total_rows, head_count, VH)
    return (scaled * gate_heads * jax.nn.sigmoid(gate_heads)).reshape(total_rows, head_count * VH)

def inv_rms(values_in):
    return lax.rsqrt(lax.optimization_barrier(jnp.mean(values_in * values_in, axis=-1, keepdims=True)) + norm_eps)

def norm_back(grad_in, normed, scale, gain):
    scaled_grad = grad_in * gain
    return scale * (scaled_grad - normed * lax.optimization_barrier(jnp.mean(scaled_grad * normed, axis=-1, keepdims=True)))

def reference(block_input, segment_ids, norm_attn, w_query, w_key, w_value, w_outgate, w_lowrank, w_forget, forget_bias, norm_group, w_output, norm_ffn, w_gate, w_up, w_down, out_grad):
    inputs_f = block_input.astype(jnp.float32)
    scale_one = inv_rms(inputs_f)
    normed_one = inputs_f * scale_one
    hidden_one = (normed_one * norm_attn).astype(jnp.bfloat16)
    queries = matmul(hidden_one, w_query).astype(jnp.bfloat16)
    key_vecs = matmul(hidden_one, w_key).astype(jnp.bfloat16)
    value_vecs = matmul(hidden_one, w_value).astype(jnp.bfloat16)
    outgate = matmul(hidden_one, w_outgate)
    lowrank = matmul(hidden_one, w_lowrank).astype(jnp.bfloat16)
    forget_logit = matmul(lowrank, w_forget) + forget_bias
    log_decay = jax.nn.log_sigmoid(forget_logit) / gate_norm

    def attend_local(query_in, key_in, value_in, decay_in):
        return attend(query_in, key_in, value_in, decay_in, segment_ids)
    mixed, pull_mixer = jax.vjp(attend_local, queries.astype(jnp.float32), key_vecs.astype(jnp.float32), value_vecs.astype(jnp.float32), log_decay)
    gated_out, pull_gate = jax.vjp(gated, mixed, outgate, norm_group)
    z_rows = gated_out.astype(jnp.bfloat16)
    mid_resid = inputs_f + matmul(z_rows, w_output)
    scale_two = inv_rms(mid_resid)
    normed_two = mid_resid * scale_two
    hidden_two = (normed_two * norm_ffn).astype(jnp.bfloat16)
    gate_pre = matmul(hidden_two, w_gate)
    up_pre = matmul(hidden_two, w_up)
    gate_sig = jax.nn.sigmoid(gate_pre)
    hid_rows = (gate_pre * gate_sig * up_pre).astype(jnp.bfloat16)
    block_output = (mid_resid + matmul(hid_rows, w_down)).astype(jnp.bfloat16)
    live_rows = segment_ids[:, None] >= 0
    grad_b = jnp.where(live_rows, out_grad, jnp.zeros_like(out_grad))
    grad_f = grad_b.astype(jnp.float32)
    grad_w_down = matmul(hid_rows.T, grad_b)
    dhid = matmul(grad_b, w_down.T)
    dgate = (dhid * up_pre * gate_sig * (1.0 + gate_pre * (1.0 - gate_sig))).astype(jnp.bfloat16)
    dup = (dhid * gate_pre * gate_sig).astype(jnp.bfloat16)
    grad_w_gate = matmul(hidden_two.T, dgate)
    grad_w_up = matmul(hidden_two.T, dup)
    dh_two = matmul(dgate, w_gate.T) + matmul(dup, w_up.T)
    grad_norm_ffn = lax.optimization_barrier(jnp.sum(dh_two * normed_two, axis=0))
    dmid = grad_f + norm_back(dh_two, normed_two, scale_two, norm_ffn)
    dmid_b = dmid.astype(jnp.bfloat16)
    grad_w_output = matmul(z_rows.T, dmid_b)
    dz_rows = matmul(dmid_b, w_output.T)
    dmixed, doutgate, grad_norm_group = pull_gate(dz_rows)
    dquery, dkey, dvalue, dlog = pull_mixer(dmixed)
    dlogit = dlog / gate_norm * jax.nn.sigmoid(-forget_logit)
    grad_forget_bias = lax.optimization_barrier(jnp.sum(dlogit, axis=0))
    dlogit_b = dlogit.astype(jnp.bfloat16)
    grad_w_forget = matmul(lowrank.T, dlogit_b)
    dlow = matmul(dlogit_b, w_forget.T)
    grad_w_lowrank = exact_matmul(hidden_one.T, dlow)
    dquery_b = dquery.astype(jnp.bfloat16)
    dkey_b = dkey.astype(jnp.bfloat16)
    dvalue_b = dvalue.astype(jnp.bfloat16)
    doutgate_b = doutgate.astype(jnp.bfloat16)
    grad_w_query = matmul(hidden_one.T, dquery_b)
    grad_w_key = matmul(hidden_one.T, dkey_b)
    grad_w_value = matmul(hidden_one.T, dvalue_b)
    grad_w_outgate = matmul(hidden_one.T, doutgate_b)
    dh_one = matmul(dquery_b, w_query.T) + matmul(dkey_b, w_key.T) + matmul(dvalue_b, w_value.T) + matmul(doutgate_b, w_outgate.T) + exact_matmul(dlow, w_lowrank.T)
    grad_norm_attn = lax.optimization_barrier(jnp.sum(dh_one * normed_one, axis=0))
    input_grad = (dmid + norm_back(dh_one, normed_one, scale_one, norm_attn)).astype(jnp.bfloat16)
    return (block_output, input_grad, grad_norm_attn, grad_w_query, grad_w_key, grad_w_value, grad_w_outgate, grad_w_lowrank, grad_w_forget, grad_forget_bias, grad_norm_group, grad_w_output, grad_norm_ffn, grad_w_gate, grad_w_up, grad_w_down)
```

```python
import functools

import jax
import jax.numpy as jnp
from jax import lax
from jax.experimental import pallas as pl
from jax.experimental.pallas import tpu as pltpu
from jax.sharding import PartitionSpec as P

KH = 128
VH = 256
CHUNK = 64

norm_eps = 1e-06
group_eps = 0.1
gate_norm = 16.0

f32 = jnp.float32
bf16 = jnp.bfloat16


def nn(a, b):
    return jnp.dot(a, b, preferred_element_type=f32)


def nt(a, b):
    return lax.dot_general(a, b, (((1,), (1,)), ((), ())), preferred_element_type=f32)


def tn(a, b):
    return lax.dot_general(a, b, (((0,), (0,)), ((), ())), preferred_element_type=f32)


def split(a):
    high = a.astype(bf16)
    return high, (a - high.astype(f32)).astype(bf16)


def vmem_call(body, outs, args, flops, name, scratch=(), scalars=()):
    size = sum(a.size * a.dtype.itemsize for a in args)
    size += sum(o.size * o.dtype.itemsize for o in outs)
    spec = pl.BlockSpec(memory_space=pltpu.VMEM)
    scalar = pl.BlockSpec(memory_space=pltpu.SMEM)
    return pl.pallas_call(
        body,
        out_shape=outs,
        in_specs=[scalar] * len(scalars) + [spec] * len(args),
        out_specs=[spec] * len(outs),
        scratch_shapes=list(scratch),
        cost_estimate=pl.CostEstimate(flops=flops, bytes_accessed=size, transcendentals=0),
        compiler_params=pltpu.CompilerParams(vmem_limit_bytes=60 * 1024 * 1024),
        name=name,
    )(*scalars, *args)


def after(value, *others):
    return lax.optimization_barrier((value, *others))[0]


def shape(dims, kind):
    return jax.ShapeDtypeStruct(dims, kind)


def level_count(rows):
    return max(1, (rows - 1).bit_length())


def row_second(rows, level):
    return ((lax.broadcasted_iota(jnp.int32, (rows, 1), 0) >> level) & 1) == 1


def same_block(row, col, level):
    return (row >> (level + 1)) == (col >> (level + 1))


def sum_mask(row, col, level):
    row_late = ((row >> level) & 1) == 1
    col_late = ((col >> level) & 1) == 1
    late = row_late & col_late & (col <= row)
    early = jnp.logical_not(row_late | col_late) & (col > row)
    return same_block(row, col, level) & (late | early)


def as_bf16(mask):
    return jnp.where(mask, 1.0, 0.0).astype(bf16)


def column_of(row_vector):
    rows = row_vector.shape[1]
    row = lax.broadcasted_iota(jnp.int32, (rows, rows), 0)
    col = lax.broadcasted_iota(jnp.int32, (rows, rows), 1)
    return jnp.sum(jnp.where(row == col, row_vector, 0.0), axis=-1, keepdims=True)


def segment_mask(seg_ref):
    rows = seg_ref.shape[0]
    line = seg_ref[...].astype(f32).reshape(1, rows)
    column = column_of(line)
    return column == line, column


def write_parts(parts, value):
    size = value.shape[0] // len(parts)
    for c, part in enumerate(parts):
        part[...] = value[c * size : (c + 1) * size]


def forward_kernel(chunks, refs):
    (x_ref, gain_ref, wq_ref, wk_ref, wv_ref, wg_ref, wl_ref, wf_ref, bias_ref, group_ref,
     seg_ref, wo_ref) = refs[:12]
    (h_ref, q_ref, k_ref, v_ref, og_ref, low_ref, logit_ref, decay_ref, mixed_ref, z_ref) = refs[12:22]
    parts = refs[22 : 22 + chunks]
    scores_ref = refs[22 + chunks]
    rows = x_ref.shape[0]
    xf = x_ref[...].astype(f32)
    scale = lax.rsqrt(jnp.mean(xf * xf, axis=-1, keepdims=True) + norm_eps)
    hidden = (xf * scale * gain_ref[...].reshape(1, -1)).astype(bf16)
    h_ref[...] = hidden
    q = nn(hidden, wq_ref[...]).astype(bf16)
    k = nn(hidden, wk_ref[...]).astype(bf16)
    v = nn(hidden, wv_ref[...]).astype(bf16)
    og = nn(hidden, wg_ref[...])
    low = nt(hidden, wl_ref[...]).astype(bf16)
    logit = nn(low, wf_ref[...]) + bias_ref[...].reshape(1, -1)
    q_ref[...] = q
    k_ref[...] = k
    v_ref[...] = v
    og_ref[...] = og
    low_ref[...] = low
    logit_ref[...] = logit
    log_decay = (jnp.minimum(logit, 0.0) - jnp.log1p(jnp.exp(-jnp.abs(logit)))) / gate_norm
    both = jnp.concatenate(split(log_decay), axis=1)
    qf = q.astype(f32) * KH ** (-0.5)
    kf = k.astype(f32)
    row = lax.broadcasted_iota(jnp.int32, (rows, rows), 0)
    col = lax.broadcasted_iota(jnp.int32, (rows, rows), 1)
    same_seg, _ = segment_mask(seg_ref)
    scores_ref[...] = jnp.zeros_like(scores_ref)

    def one(level, carry):
        halves = nn(as_bf16(sum_mask(row, col, level)), both)
        decay = jnp.exp(halves[:, :KH] + halves[:, KH:])
        decay_ref[level] = decay
        late = row_second(rows, level)
        qs = jnp.where(late, qf * decay, 0.0).astype(bf16)
        ks = jnp.where(late, 0.0, kf * decay).astype(bf16)
        scores_ref[...] += jnp.where(same_block(row, col, level), nt(qs, ks), 0.0)
        return carry

    lax.fori_loop(0, level_count(rows), one, 0)
    scores = jnp.where(same_seg, scores_ref[...], 0.0).astype(bf16)
    diagonal = jnp.sum(qf * kf, axis=-1, keepdims=True)
    mixed = nn(scores, v) + diagonal * v.astype(f32)
    mixed_ref[...] = mixed
    inv = lax.rsqrt(jnp.mean(mixed * mixed, axis=-1, keepdims=True) + group_eps)
    z = (mixed * inv * group_ref[...].reshape(1, -1) * og * jax.nn.sigmoid(og)).astype(bf16)
    z_ref[...] = z
    write_parts(parts, nn(z, wo_ref[...]))


def ffn_kernel(chunks, refs):
    x_ref, inner_ref = refs[:2]
    mine = refs[2 : 2 + chunks]
    sent = refs[2 + chunks : 2 + 2 * chunks]
    gain_ref, wg_ref, wu_ref, dhid_ref = refs[2 + 2 * chunks : 6 + 2 * chunks]
    x1_ref, h_ref, hid_ref, dgate_ref, dup_ref = refs[6 + 2 * chunks : 11 + 2 * chunks]
    parts = refs[11 + 2 * chunks :]
    inner = inner_ref[...] > 0.5
    total = jnp.concatenate(
        [jnp.where(inner, mine[c][...], sent[c][...]) for c in range(chunks)], axis=0
    )
    x1 = x_ref[...].astype(f32) + total
    x1_ref[...] = x1
    scale = lax.rsqrt(jnp.mean(x1 * x1, axis=-1, keepdims=True) + norm_eps)
    hidden = (x1 * scale * gain_ref[...].reshape(1, -1)).astype(bf16)
    h_ref[...] = hidden
    gate = nt(hidden, wg_ref[...])
    up = nt(hidden, wu_ref[...])
    sig = jax.nn.sigmoid(gate)
    hid_ref[...] = (gate * sig * up).astype(bf16)
    dhid = dhid_ref[...]
    dgate = (dhid * up * sig * (1.0 + gate * (1.0 - sig))).astype(bf16)
    dup = (dhid * gate * sig).astype(bf16)
    dgate_ref[...] = dgate
    dup_ref[...] = dup
    write_parts(parts, nn(dgate, wg_ref[...]) + nn(dup, wu_ref[...]))


def down_kernel(refs):
    hid_ref, wd_ref, *parts = refs
    write_parts(parts, nn(hid_ref[...], wd_ref[...]))


def dhid_kernel(refs):
    seg_ref, grad_ref, wd_ref, gy_ref, dhid_ref = refs
    _, column = segment_mask(seg_ref)
    gy = jnp.where(column >= 0.0, grad_ref[...].astype(f32), 0.0).astype(bf16)
    gy_ref[...] = gy
    dhid_ref[...] = nt(gy, wd_ref[...])


def backward_kernel(chunks, refs):
    inner_ref = refs[0]
    mine = refs[1 : 1 + chunks]
    sent = refs[1 + chunks : 1 + 2 * chunks]
    (x_ref, x1_ref, h_ref, gy_ref, gain_ref, group_ref, q_ref, k_ref, v_ref, og_ref, low_ref,
     logit_ref, decay_ref, mixed_ref, seg_ref, wq_ref, wk_ref, wv_ref, wg_ref, wl_ref,
     wf_ref, wo_ref) = refs[1 + 2 * chunks : 23 + 2 * chunks]
    (dmid_ref, dmidb_ref, dq_ref, dk_ref, dv_ref, dog_ref, shared_ref, local_ref) = refs[
        23 + 2 * chunks : 31 + 2 * chunks
    ]
    parts = refs[31 + 2 * chunks : 31 + 3 * chunks]
    dscore_ref, dscore_t_ref, scores_ref, dqa_ref, dka_ref, dlog_ref = refs[31 + 3 * chunks :]
    rows = x_ref.shape[0]
    wide = x_ref.shape[1]
    inner = inner_ref[...] > 0.5
    dh2 = jnp.concatenate(
        [jnp.where(inner, mine[c][...], sent[c][...]) for c in range(chunks)], axis=0
    )
    x1 = x1_ref[...]
    scale = lax.rsqrt(jnp.mean(x1 * x1, axis=-1, keepdims=True) + norm_eps)
    normed = x1 * scale
    ffn_gain = jnp.sum(dh2 * normed, axis=0, keepdims=True)
    scaled = dh2 * gain_ref[...].reshape(1, -1)
    dmid = gy_ref[...].astype(f32) + scale * (
        scaled - normed * jnp.mean(scaled * normed, axis=-1, keepdims=True)
    )
    dmid_ref[...] = dmid
    dmid_b = dmid.astype(bf16)
    dmidb_ref[...] = dmid_b
    dz = nt(dmid_b, wo_ref[...])
    mixed = mixed_ref[...]
    og = og_ref[...]
    sig = jax.nn.sigmoid(og)
    inv = lax.rsqrt(jnp.mean(mixed * mixed, axis=-1, keepdims=True) + group_eps)
    unit = mixed * inv
    dscaled = dz * og * sig
    group = group_ref[...].reshape(1, -1)
    dog = (dz * unit * group * sig * (1.0 + og * (1.0 - sig))).astype(bf16)
    dog_ref[...] = dog
    group_part = jnp.sum(dscaled * unit, axis=0, keepdims=True)
    dunit = dscaled * group
    dmixed = inv * (dunit - unit * jnp.mean(dunit * unit, axis=-1, keepdims=True))
    qf = q_ref[...].astype(f32) * KH ** (-0.5)
    kf = k_ref[...].astype(f32)
    v = v_ref[...]
    vf = v.astype(f32)
    out_b = dmixed.astype(bf16)
    row = lax.broadcasted_iota(jnp.int32, (rows, rows), 0)
    col = lax.broadcasted_iota(jnp.int32, (rows, rows), 1)
    same_seg, _ = segment_mask(seg_ref)
    dscore_ref[...] = jnp.where(same_seg, nt(out_b, v), 0.0)
    dscore_t_ref[...] = jnp.where(same_seg, nt(v, out_b), 0.0)
    diagonal = jnp.sum(qf * kf, axis=-1, keepdims=True)
    ddiagonal = jnp.sum(dmixed * vf, axis=-1, keepdims=True)
    dqa_ref[...] = ddiagonal * kf
    dka_ref[...] = ddiagonal * qf
    dlog_ref[...] = jnp.zeros_like(dlog_ref)
    scores_ref[...] = jnp.zeros_like(scores_ref)

    def one(level, carry):
        decay = decay_ref[level]
        late = row_second(rows, level)
        qs = jnp.where(late, qf * decay, 0.0)
        ks = jnp.where(late, 0.0, kf * decay)
        qs_b = qs.astype(bf16)
        ks_b = ks.astype(bf16)
        near = same_block(row, col, level)
        dqs = jnp.where(late, nn(jnp.where(near, dscore_ref[...], 0.0).astype(bf16), ks_b), 0.0)
        dks = jnp.where(late, 0.0, nn(jnp.where(near, dscore_t_ref[...], 0.0).astype(bf16), qs_b))
        scores_ref[...] += jnp.where(near, nt(ks_b, qs_b), 0.0)
        dqa_ref[...] += dqs * decay
        dka_ref[...] += dks * decay
        slope = jnp.concatenate(split(qs * dqs + ks * dks), axis=1)
        halves = nn(as_bf16(sum_mask(col, row, level)), slope)
        dlog_ref[...] += halves[:, :KH] + halves[:, KH:]
        return carry

    for level in range(level_count(rows)):
        one(level, 0)
    dq = dqa_ref[...]
    dk = dka_ref[...]
    dlog = dlog_ref[...]
    scores_t = jnp.where(same_seg, scores_ref[...], 0.0).astype(bf16)
    dv = nn(scores_t, out_b) + diagonal * dmixed
    dq_b = (dq * KH ** (-0.5)).astype(bf16)
    dk_b = dk.astype(bf16)
    dv_b = dv.astype(bf16)
    dq_ref[...] = dq_b
    dk_ref[...] = dk_b
    dv_ref[...] = dv_b
    logit = logit_ref[...]
    dlogit = dlog / gate_norm * jax.nn.sigmoid(-logit)
    dlogit_b = dlogit.astype(bf16)
    rank = low_ref.shape[1]
    local_ref[...] = jnp.zeros_like(local_ref)
    local_ref[0:rank, :] = tn(low_ref[...], dlogit_b)
    local_ref[rank : rank + 1, :] = jnp.sum(dlogit, axis=0, keepdims=True)
    for j in range(wide // 128):
        local_ref[rank + 8 + j : rank + 9 + j, :] = ffn_gain[:, j * 128 : (j + 1) * 128]
    low_high, low_low = split(nt(dlogit_b, wf_ref[...]))
    xf = x_ref[...].astype(f32)
    first = lax.rsqrt(jnp.mean(xf * xf, axis=-1, keepdims=True) + norm_eps)
    dh = (
        nt(dq_b, wq_ref[...])
        + nt(dk_b, wk_ref[...])
        + nt(dv_b, wv_ref[...])
        + nt(dog, wg_ref[...])
        + nn(low_high, wl_ref[...])
        + nn(low_low, wl_ref[...])
    )
    write_parts(parts, dh)
    attn_gain = jnp.sum(dh * (xf * first), axis=0, keepdims=True)
    hidden = h_ref[...]
    low_rank = tn(low_high, hidden) + tn(low_low, hidden)
    shared_ref[...] = jnp.zeros_like(shared_ref)
    for j in range(wide // 128):
        cols = slice(j * 128, (j + 1) * 128)
        shared_ref[j * rank : (j + 1) * rank, :] = low_rank[:, cols]
        base = rank * (wide // 128)
        shared_ref[base + j : base + j + 1, :] = attn_gain[:, cols]
    base = (rank + 1) * (wide // 128)
    for j in range(VH // 128):
        shared_ref[base + j : base + j + 1, :] = group_part[:, j * 128 : (j + 1) * 128]


def pick_kernel(refs):
    *pairs, inner_ref, extra_ref, o_ref = refs
    half = len(pairs) // 2
    inner = inner_ref[...] > 0.5
    total = jnp.concatenate(
        [jnp.where(inner, pairs[c][...], pairs[half + c][...]) for c in range(half)], axis=0
    )
    o_ref[...] = (extra_ref[...] + total).astype(bf16)


def final_kernel(chunks, refs):
    inner_ref = refs[0]
    mine = refs[1 : 1 + chunks]
    sent = refs[1 + chunks : 1 + 2 * chunks]
    x_ref, dmid_ref, gain_ref, o_ref = refs[1 + 2 * chunks :]
    inner = inner_ref[...] > 0.5
    dh = jnp.concatenate(
        [jnp.where(inner, mine[c][...], sent[c][...]) for c in range(chunks)], axis=0
    )
    xf = x_ref[...].astype(f32)
    scale = lax.rsqrt(jnp.mean(xf * xf, axis=-1, keepdims=True) + norm_eps)
    normed = xf * scale
    scaled = dh * gain_ref[...].reshape(1, -1)
    o_ref[...] = (
        dmid_ref[...]
        + scale * (scaled - normed * jnp.mean(scaled * normed, axis=-1, keepdims=True))
    ).astype(bf16)


def packed(body, *fixed):
    return lambda *refs: body(*fixed, refs)


class LineSum:
    def __init__(self, parts, axis, name):
        self.parts, self.axis, self.name = list(parts), axis, name
        self.count = len(self.parts)
        self.got, self.pairs, self.across, self.totals, self.sent = [], [], [], [], []

    def move(self, value, perm, stage, c):
        with jax.named_scope(f"{self.name}_{stage}{c}"):
            return lax.ppermute(value, self.axis, perm)

    def begin(self):
        for c, part in enumerate(self.parts):
            self.got.append(self.move(part, [(0, 1), (3, 2)], "in", c))

    def pair(self, c, token):
        got, part, *_ = lax.optimization_barrier((self.got[c], self.parts[c], *token))
        value = part + got
        self.pairs.append(value)
        self.across.append(self.move(value, [(1, 2), (2, 1)], "ex", c))
        return (value,)

    def total(self, c, token):
        got, pair, *_ = lax.optimization_barrier((self.across[c], self.pairs[c], *token))
        value = pair + got
        self.totals.append(value)
        self.sent.append(self.move(value, [(1, 0), (2, 3)], "out", c))
        return (value,)

    def run(self, token=()):
        for c in range(self.count):
            token = self.pair(c, token)
            if c:
                token = self.total(c - 1, token)
        return self.total(self.count - 1, token)


def swap(value, axis, count, bit):
    return lax.ppermute(value, axis, [(i, i ^ bit) for i in range(count)])


def bit_of(index, bit):
    return (index // bit) % 2


def product_kernel(plan, refs):
    core_ref = refs[0]
    count = 1 + max(max(p[0], p[1]) for p in plan)
    operands = refs[1 : 1 + count]
    kept_ref, away_ref, whole_ref = refs[1 + count :]
    core = core_ref[0]
    for left, right, group, start in plan:
        value = tn(operands[left][...], operands[right][...])
        columns = value.shape[1]
        whole_ref[:, :, :, 0:columns] = value.reshape(whole_ref.shape[:3] + (columns,))
        for i in range(whole_ref.shape[0]):
            kept_ref[group, i, :, start : start + columns] = whole_ref[i, core, :, 0:columns]
            away_ref[group, i, :, start : start + columns] = whole_ref[i, 1 - core, :, 0:columns]


def fold_kernel(views, refs):
    which_ref = refs[0]
    ins = refs[1 : 1 + 2 * len(views)]
    outs = refs[1 + 2 * len(views) :]
    for color, (outer, inside, start, size) in enumerate(views):
        a_ref, b_ref = ins[2 * color : 2 * color + 2]
        kept_ref, away_ref = outs[2 * color : 2 * color + 2]
        mine = which_ref[color]
        span = slice(start, start + size)
        for i in range(outer):
            for j in range(inside):
                kept_ref[i * inside + j] = a_ref[i, mine, j, span] + b_ref[i, mine, j, span]
                away_ref[i * inside + j] = a_ref[i, 1 - mine, j, span] + b_ref[i, 1 - mine, j, span]


def last_kernel(plan, refs):
    a0, b0, a1, b1 = refs[:4]
    half = a0.shape[1]
    for out, (group, start) in zip(refs[4:], plan):
        columns = out.shape[1]
        out[0:half, :] = a0[group, :, start : start + columns] + b0[group, :, start : start + columns]
        out[half:, :] = a1[group, :, start : start + columns] + b1[group, :, start : start + columns]


class Scatter:
    def __init__(self, dp, index, name):
        self.dp, self.index, self.name = dp, index, name
        self.bits = [1 << b for b in range(1, (dp - 1).bit_length())]

    def products(self, operands, plan, groups, columns):
        wide = operands[0].shape[1]
        rows = operands[0].shape[0]
        self.block = wide // self.dp
        self.groups, self.columns = groups, columns
        half = self.dp // 2
        out = shape((groups, half, self.block, columns), f32)
        widest = max(operands[p[1]].shape[1] for p in plan)
        core = bit_of(self.index, 1).reshape(1)
        flops = sum(2 * rows * wide * operands[p[1]].shape[1] for p in plan)
        self.kept, away = vmem_call(
            packed(product_kernel, plan), [out, out], operands, flops, f"{self.name}_product",
            scratch=[pltpu.VMEM((half, 2, self.block, widest), f32)], scalars=[core],
        )
        with jax.named_scope(f"{self.name}_b1"):
            self.got = swap(away, "dp", self.dp, 1)

    def run(self):
        bits, block, columns = self.bits, self.block, self.columns
        turn = len(bits) // 2
        orders = [bits, bits[turn:] + bits[:turn]]
        left = [bits[::-1], bits[::-1]]
        pairs = [(self.kept, self.got)] * 2
        for step in range(len(bits)):
            views, args, outs, which = [], [], [], []
            for color in range(2):
                b = orders[color][step]
                at = left[color].index(b)
                outer = self.groups << at
                inside = 1 << (len(left[color]) - at - 1)
                tall = block if step == 0 else block // 2
                start = color * (block // 2) if step == 0 else 0
                views.append((outer, inside, start, block // 2))
                args += [p.reshape(outer, 2, inside, tall, columns) for p in pairs[color]]
                outs += [shape((outer * inside, block // 2, columns), f32)] * 2
                which.append(bit_of(self.index, b))
                left[color] = [x for x in left[color] if x != b]
            results = vmem_call(
                packed(fold_kernel, views), outs, args, self.kept.size, f"{self.name}_fold{step}",
                scalars=[jnp.stack(which)],
            )
            pairs = []
            for color in range(2):
                b = orders[color][step]
                with jax.named_scope(f"{self.name}_c{color}_b{b}"):
                    arrived = swap(results[2 * color + 1], "dp", self.dp, b)
                pairs.append((results[2 * color], arrived))
        self.pairs = pairs

    def finish(self, plan):
        args = [p for pair in self.pairs for p in pair]
        outs = [shape((self.block, columns), f32) for _, _, columns in plan]
        return vmem_call(
            packed(last_kernel, [p[:2] for p in plan]), outs, args, args[0].size, f"{self.name}_last"
        )


def doubling(value, axis, count, name):
    b = 1
    while b < count:
        with jax.named_scope(f"{name}_{b}"):
            value = value + swap(value, axis, count, b)
        b *= 2
    return value


def on_device(
    dp,
    tensor,
    block_input,
    segment_ids,
    norm_attn,
    w_query,
    w_key,
    w_value,
    w_outgate,
    w_lowrank,
    w_forget,
    forget_bias,
    norm_group,
    w_output,
    norm_ffn,
    w_gate,
    w_up,
    w_down,
    out_grad,
):
    rows, wide = block_input.shape
    hidden_units = w_gate.shape[1]
    rank = w_lowrank.shape[1]
    chunks = rows // CHUNK
    t_index = lax.axis_index("tensor")
    d_index = lax.axis_index("dp")
    inner = jnp.where((t_index == 1) | (t_index == 2), 1.0, 0.0).astype(f32).reshape(1, 1)
    piece = shape((CHUNK, wide), f32)
    levels = level_count(rows)
    w_lowrank, w_gate, w_up = w_lowrank.T, w_gate.T, w_up.T
    square = pltpu.VMEM((rows, rows), f32)
    key_rows = pltpu.VMEM((rows, KH), f32)

    outs = [
        shape((rows, wide), bf16),
        shape((rows, KH), bf16),
        shape((rows, KH), bf16),
        shape((rows, VH), bf16),
        shape((rows, VH), f32),
        shape((rows, rank), bf16),
        shape((rows, KH), f32),
        shape((levels, rows, KH), f32),
        shape((rows, VH), f32),
        shape((rows, VH), bf16),
    ] + [piece] * chunks
    h1, q, k, v, og, low, logit, decay, mixed, z, *parts = vmem_call(
        packed(forward_kernel, chunks),
        outs,
        [block_input, norm_attn, w_query, w_key, w_value, w_outgate, w_lowrank, w_forget,
         forget_bias, norm_group, segment_ids, w_output],
        2 * rows * wide * 1024,
        "mix_forward",
        scratch=[square],
    )
    first = LineSum(parts, "tensor", "mixsum")
    first.begin()
    gy, dhid = vmem_call(
        packed(dhid_kernel),
        [shape((rows, wide), bf16), shape((rows, hidden_units), f32)],
        [segment_ids, out_grad, w_down],
        2 * rows * wide * hidden_units,
        "dhid",
    )
    first.run()

    outs = [
        shape((rows, wide), f32),
        shape((rows, wide), bf16),
        shape((rows, hidden_units), bf16),
        shape((rows, hidden_units), bf16),
        shape((rows, hidden_units), bf16),
    ] + [piece] * chunks
    x1, h2, hid, dgate, dup, *parts = vmem_call(
        packed(ffn_kernel, chunks),
        outs,
        [block_input, inner, *first.totals, *first.sent, norm_ffn, w_gate, w_up, dhid],
        8 * rows * wide * hidden_units,
        "ffn",
    )
    third = LineSum(parts, "tensor", "dhsum")
    third.begin()
    ffn_grads = Scatter(dp, d_index, "ffnw")
    ffn_grads.products(
        [h2, gy, dgate, dup, hid], [(0, 2, 0, 0), (0, 3, 1, 0), (1, 4, 2, 0)], 3, hidden_units
    )
    parts = vmem_call(
        packed(down_kernel), [piece] * chunks, [hid, w_down], 2 * rows * wide * hidden_units, "down"
    )
    token = third.run()
    second = LineSum([after(p, *third.pairs) for p in parts], "tensor", "ffnsum")
    second.begin()
    ffn_grads.run()

    outs = [
        shape((rows, wide), f32),
        shape((rows, wide), bf16),
        shape((rows, KH), bf16),
        shape((rows, KH), bf16),
        shape((rows, VH), bf16),
        shape((rows, VH), bf16),
        shape(((rank + 1) * (wide // 128) + 8, 128), f32),
        shape((rank + 8 + wide // 128, 128), f32),
    ] + [piece] * chunks
    dmid, dmid_b, dq, dk, dv, dog, shared, local, *parts = vmem_call(
        packed(backward_kernel, chunks),
        outs,
        [inner, *third.totals, *third.sent, block_input, x1, h1, gy, norm_ffn, norm_group, q, k, v,
         og, low, logit, decay, mixed, segment_ids, w_query, w_key, w_value, w_outgate, w_lowrank,
         w_forget, w_output],
        2 * rows * wide * 2048,
        "mix_backward",
        scratch=[square] * 3 + [key_rows] * 3,
    )
    fourth = LineSum(parts, "tensor", "gradsum")
    fourth.begin()
    mix_grads = Scatter(dp, d_index, "mixw")
    mix_grads.products(
        [h1, dmid_b, dq, dk, dv, dog, z],
        [(0, 2, 0, 0), (0, 3, 0, KH), (0, 4, 0, 2 * KH), (0, 5, 0, 2 * KH + VH),
         (1, 6, 0, 2 * KH + 2 * VH)],
        1,
        2 * KH + 3 * VH,
    )
    token = second.run()
    token = fourth.run(token)
    mix_grads.run()
    g_gate, g_up, g_down = ffn_grads.finish([(g, 0, hidden_units) for g in range(3)])
    g_query, g_key, g_value, g_outgate, g_output = mix_grads.finish(
        [(0, 0, KH), (0, KH, KH), (0, 2 * KH, VH), (0, 2 * KH + VH, VH), (0, 2 * KH + 2 * VH, VH)]
    )

    small = jnp.concatenate([shared, local], axis=0)
    small = doubling(small, "dp", dp, "small")
    count = shared.shape[0]
    local = small[count:]
    shared = doubling(small[:count], "tensor", tensor, "smallt")
    groups = wide // 128

    def own(vector):
        size = vector.shape[0] // dp
        return lax.dynamic_slice_in_dim(vector, d_index * size, size, 0)

    low_rank = shared[: rank * groups].reshape(groups, rank, 128).transpose(0, 2, 1)
    g_lowrank = own(low_rank.reshape(wide, rank))
    g_norm_attn = own(shared[rank * groups : (rank + 1) * groups].reshape(wide))
    base = (rank + 1) * groups
    g_group = own(shared[base : base + VH // 128].reshape(VH))
    g_forget = local[:rank]
    g_bias = local[rank]
    g_norm_ffn = own(local[rank + 8 : rank + 8 + groups].reshape(wide))

    block_output = vmem_call(
        lambda *refs: pick_kernel(refs),
        [shape((rows, wide), bf16)],
        [*second.totals, *second.sent, inner, x1],
        rows * wide,
        "block_out",
    )[0]
    input_grad = vmem_call(
        packed(final_kernel, chunks),
        [shape((rows, wide), bf16)],
        [inner, *fourth.totals, *fourth.sent, block_input, dmid, norm_attn],
        rows * wide,
        "input_grad",
    )[0]
    return (
        block_output,
        input_grad,
        g_norm_attn,
        g_query,
        g_key,
        g_value,
        g_outgate,
        g_lowrank,
        g_forget,
        g_bias,
        g_group,
        g_output.T,
        g_norm_ffn,
        g_gate,
        g_up,
        g_down.T,
    )


def solution(mesh):
    in_specs = (
        P("dp", None),
        P("dp"),
        P(),
        P(None, "tensor"),
        P(None, "tensor"),
        P(None, "tensor"),
        P(None, "tensor"),
        P(),
        P(None, "tensor"),
        P("tensor"),
        P(),
        P("tensor", None),
        P(),
        P(None, "tensor"),
        P(None, "tensor"),
        P("tensor", None),
        P("dp", None),
    )
    out_specs = (
        P("dp", None),
        P("dp", None),
        P("dp"),
        P("dp", "tensor"),
        P("dp", "tensor"),
        P("dp", "tensor"),
        P("dp", "tensor"),
        P("dp", None),
        P(None, "tensor"),
        P("tensor"),
        P("dp"),
        P("tensor", "dp"),
        P("dp"),
        P("dp", "tensor"),
        P("dp", "tensor"),
        P("tensor", "dp"),
    )
    body = functools.partial(on_device, mesh.shape["dp"], mesh.shape["tensor"])
    return jax.shard_map(body, mesh=mesh, in_specs=in_specs, out_specs=out_specs, check_vma=False)
```
